512 devices in a mesh: tile: 64 (over z, x, core), tm: 8 (over y).
Axes of the slice: x: 4, y: 8, z: 8, core: 2. Of those that a mesh axis runs over, the one named last changes fastest.
Arguments:
- data: bfloat16 [8192, 64, 128], P('tile', 'tm'), may hold values from -8 to 8
- send_list: int32 [64, 64, 8], P('tile'), may hold values from 0 to 127
- footprint_slot: int32 [8192, 8], P('tile'), may hold values from 0 to 511, as said below
- footprint: bfloat16 [8192, 8, 128], P('tile'), may hold values from 0 to 0.053955078
- colour: int32 [8192], P('tile'), may hold values from 0 to 3, as said below
- correlation: int32 [8192, 8], P('tile'), may hold values from 0 to 8191, as said below
- correlation_gram: float32 [8192, 8], P('tile'), may hold values from 0.01 to 0.15
- traces_init: float32 [64, 8192], P('tm', 'tile'), may hold values from 0 to 4
Outputs:
- traces: float32 [64, 8192], P('tm', 'tile')
- trace_rms: float32 [8192], P('tile')
The draws below stay inside these ranges and needn't reach their ends.
Inputs may be any that keep to these rules, and one draw needn't show every extreme that they name: footprint_slot[k, j] names the slot c = footprint_slot[k, j] % 8 in which tile device footprint_slot[k, j] // 8 sends a block to the owner of k, tile device k // 128; the 8 slots of one footprint differ. Each tile device owns exactly a quarter of its 128 components in each colour; every listed neighbour has a colour other than the component's own. `correlation`: the tile axis folds the slab's two halves end to end, so the neighbours of a component owned by tile device d are owned by tile device d - 1, d, d + 1 or (d + 32) modulo 64; entries may repeat.
All inputs are finite; a program needn't handle non-finite values.
Results may differ from the reference program's by a relative error of at most 0.0003.
Values may be sent and summed in bfloat16 or wider, within the bound.
A program may use at most 64 MiB of HBM per device.

```python
import math
import jax
import jax.numpy as jnp
from jax import lax

VOX = 128
VB_DEV = 128
K_DEV = 128
FPB = 8
CAP = 8
OV = 8
NBLK = 8192
FRAMES = 64
K = 8192
SLOTS = 512
N_TILE = 64


def colour_plan(key):
    tiles_all = K // K_DEV
    quarter = K_DEV // 4
    scores = jax.random.randint(jax.random.fold_in(key, 1), (tiles_all, K_DEV), 0, 2 ** 20)
    scores = scores * K_DEV + jnp.arange(K_DEV, dtype=jnp.int32)[None, :]
    sorted_index = jnp.argsort(scores, axis=1).astype(jnp.int32)
    positions = jnp.argsort(sorted_index, axis=1).astype(jnp.int32)
    colours = (positions % 4).reshape(K)
    owner_dev = jnp.arange(K, dtype=jnp.int32) // K_DEV
    offsets = jax.random.randint(jax.random.fold_in(key, 2), (K, OV), -1, 2)
    near_target = jnp.clip(owner_dev[:, None] + offsets, 0, tiles_all - 1)
    far_target = (owner_dev[:, None] + tiles_all // 2) % tiles_all
    column_ids = jnp.arange(OV, dtype=jnp.int32)[None, :]
    target = jnp.where(column_ids == OV - 1, far_target, near_target)
    shifts = jax.random.randint(jax.random.fold_in(key, 3), (K, OV), 1, 4)
    wanted = (colours[:, None] + shifts) % 4
    member = jax.random.randint(jax.random.fold_in(key, 4), (K, OV), 0, quarter)
    local_index = sorted_index[target, 4 * member + wanted]
    neighbour_ids = target * K_DEV + local_index
    return (colours.astype(jnp.int32), neighbour_ids.astype(jnp.int32))


def draw_colour(key, part):
    return colour_plan(jax.random.fold_in(key, 7))[0]


def draw_correlation(key, part):
    return colour_plan(jax.random.fold_in(key, 7))[1]


def draw_footprint_slot(key, part):
    band_size = SLOTS // FPB
    picked = jax.random.randint(key, (K, FPB), 0, band_size)
    return (picked + jnp.arange(FPB, dtype=jnp.int32)[None, :] * band_size).astype(jnp.int32)


def draw_data(key, part):
    first_key, second_key = jax.random.split(key)
    frame_pos = jnp.arange(FRAMES, dtype=jnp.float32)
    bleach = jnp.exp(-1.2 * frame_pos / FRAMES)[None, :, None]
    bright = jax.random.uniform(first_key, (NBLK, 1, 1), jnp.float32, 0.5, 2.0)
    noise = jax.random.truncated_normal(second_key, -3.5, 3.5, (NBLK, FRAMES, VOX), jnp.float32)
    return (bleach * bright * (0.1 + noise)).astype(jnp.bfloat16)


def place_ends(result, own_key, smallest, high):
    dims = result.shape
    place = [jax.random.randint(jax.random.fold_in(own_key, axis), (), 0, dims[axis]) for axis in range(len(dims))]
    result = result.at[tuple(place)].set(smallest)
    longest = dims.index(max(dims))
    place[longest] = (place[longest] + 1) % dims[longest]
    return result.at[tuple(place)].set(high)


def levels(rng, shape, cuts, least, top_value):
    loudness = 1.0
    for axis_at, shards_of in cuts:
        heights = jax.random.uniform(jax.random.fold_in(jax.random.fold_in(rng, 6), axis_at), (shards_of,), jnp.float32, least / len(cuts), top_value / len(cuts))
        loudness = loudness * jnp.repeat(jnp.exp(heights), shape[axis_at] // shards_of).reshape((-1,) + (1,) * (len(shape) - 1 - axis_at))
    return loudness


def setup_inputs(seed: int = 0) -> dict:
    splits = jax.random.split(jax.random.key(seed), 9)
    return {
        "data": draw_data(jax.random.fold_in(splits[8], 71), 0),
        "send_list": place_ends(jax.random.randint(splits[1], (N_TILE, N_TILE, CAP), 0, VB_DEV), jax.random.fold_in(splits[1], 1), 0, VB_DEV - 1).astype(jnp.int32),
        "footprint_slot": draw_footprint_slot(jax.random.fold_in(splits[8], 71), 0),
        "footprint": jnp.clip(0.053955078 * jax.random.uniform(splits[3], (K, FPB, VOX), jnp.float32) ** levels(splits[3], (K, FPB, VOX), ((0, 64),), -0.2, 0.2), 0.0, 0.053955078).astype(jnp.bfloat16),
        "colour": draw_colour(jax.random.fold_in(splits[8], 71), 0),
        "correlation": draw_correlation(jax.random.fold_in(splits[8], 71), 0),
        "correlation_gram": jnp.clip(jnp.exp(math.log(0.15) - 2.7080503 * jax.random.uniform(splits[6], (K, OV), jnp.float32) ** levels(splits[6], (K, OV), ((0, 64),), -0.2, 0.2)), 0.01, 0.15),
        "traces_init": jnp.clip(4.0 * jax.random.uniform(splits[7], (FRAMES, K), jnp.float32) ** levels(splits[7], (FRAMES, K), ((0, 8), (1, 64)), -0.2, 0.2), 0.0, 4.0),
    }


def reference(data, send_list, footprint_slot, footprint, colour, correlation, correlation_gram, traces_init):
    owner_dev = (jnp.arange(K, dtype=jnp.int32) // K_DEV).astype(jnp.int32)
    source = (footprint_slot // CAP).astype(jnp.int32)
    slot_pos = (footprint_slot % CAP).astype(jnp.int32)
    local_block = send_list[source, owner_dev[:, None], slot_pos]
    block_id = (source * VB_DEV + local_block).astype(jnp.int32)
    weights32 = footprint.astype(jnp.float32)
    self_gram = lax.optimization_barrier(jnp.sum(weights32 * weights32, axis=(1, 2)))

    def project(inputs):
        block_rows, weight_rows = inputs
        picked = data[block_rows].astype(jnp.float32)
        return jnp.einsum('kjtv,kjv->tk', picked, weight_rows.astype(jnp.float32))
    batches = K // K_DEV
    pieces = lax.map(project, (block_id.reshape(batches, K_DEV, FPB), footprint.reshape(batches, K_DEV, FPB, VOX)))
    projected = jnp.transpose(pieces, (1, 0, 2)).reshape(FRAMES, K)
    traces = traces_init
    for step_colour in range(4):
        neighbour_sum = jnp.zeros((FRAMES, K), jnp.float32)
        for column in range(OV):
            neighbour_sum = neighbour_sum + correlation_gram[:, column][None, :] * traces[:, correlation[:, column]]
        fresh = jnp.maximum((projected - neighbour_sum) / self_gram[None, :], 0.0)
        traces = jnp.where((colour == step_colour)[None, :], fresh, traces)
    trace_rms = jnp.sqrt(lax.optimization_barrier(jnp.mean(traces * traces, axis=0)) + 1e-06)
    return (traces, trace_rms)
```

```python
import functools

import jax
import jax.numpy as jnp
from jax import lax
from jax.experimental import pallas as pl
from jax.experimental.pallas import tpu as pltpu
from jax.sharding import PartitionSpec as P

MESH = pl.DeviceIdType.MESH
COLOURS = 4
STRIDE = 27


def sweep_kernel(
    tiles, groups, data, send, slots, footprint, colour, correlation, gram, init,
    traces_out, rms_out, outgoing, arrived, table, mine, parts,
    block_send, block_recv, near_send, near_recv, part_send, part_recv,
):
    me = lax.axis_index("tile")
    row = lax.axis_index("tm")
    cap = send.shape[0]
    blocks_fp, comps = slots.shape
    frames_dev, voxels = data.shape[1:]
    listed = correlation.shape[0]
    left = lax.rem(me + tiles - 1, tiles)
    right = lax.rem(me + 1, tiles)
    far = lax.rem(me + tiles // 2, tiles)

    barrier = pltpu.get_barrier_semaphore()

    def greet_tile(step, carry):
        peer = lax.rem(me + step * STRIDE, tiles)
        pl.semaphore_signal(barrier, inc=1, device_id={"tile": peer}, device_id_type=MESH)
        return carry

    def greet_row(step, carry):
        peer = lax.rem(row + step, groups)
        pl.semaphore_signal(barrier, inc=1, device_id={"tm": peer}, device_id_type=MESH)
        return carry

    lax.fori_loop(1, tiles, greet_tile, 0)
    lax.fori_loop(1, groups, greet_row, 0)

    def collect(owner, carry):
        for slot in range(cap):
            outgoing[owner * cap + slot] = data[send[slot, owner]]
        return carry

    lax.fori_loop(0, tiles, collect, 0)
    for slot in range(cap):
        arrived[me * cap + slot] = outgoing[me * cap + slot]

    pl.semaphore_wait(barrier, tiles - 1 + groups - 1)

    def near_copies(source, version):
        return [
            pltpu.make_async_remote_copy(
                src_ref=source,
                dst_ref=table.at[version, region],
                send_sem=near_send.at[version, region],
                recv_sem=near_recv.at[version, region],
                device_id={"tile": peer},
                device_id_type=MESH,
            )
            for region, peer in ((2, far), (0, right), (1, left))
        ]

    def block_copy(step):
        peer = lax.rem(me + step * STRIDE, tiles)
        return pltpu.make_async_remote_copy(
            src_ref=outgoing.at[pl.ds(peer * cap, cap)],
            dst_ref=arrived.at[pl.ds(me * cap, cap)],
            send_sem=block_send.at[peer],
            recv_sem=block_recv.at[me],
            device_id={"tile": peer},
            device_id_type=MESH,
        )

    def block_start(step, carry):
        block_copy(step).start()
        return carry

    lax.fori_loop(1, tiles, block_start, 0)
    copies = near_copies(init, 0)
    for copy in copies:
        copy.start()

    lane = lax.broadcasted_iota(jnp.int32, (frames_dev, comps), 1)
    zero = jnp.zeros((frames_dev, comps), jnp.float32)
    unroll = 8

    def square(step, total):
        for inner in range(unroll):
            comp = step * unroll + inner
            weights = footprint[comp].astype(jnp.float32)
            column = jnp.sum(weights * weights, axis=1, keepdims=True)
            total = jnp.where(lane == comp, column, total)
        return total

    squares = lax.fori_loop(0, comps // unroll, square, zero)
    self_gram = jnp.broadcast_to(jnp.sum(squares, axis=0, keepdims=True), zero.shape)
    ids = correlation[...]
    owner = lax.shift_right_logical(ids, comps.bit_length() - 1)
    local = ids & (comps - 1)
    code = jnp.where(owner == left, 0, jnp.where(owner == right, 1, jnp.where(owner == far, 2, 3)))
    coupling = gram[...]

    def spread(values, entry):
        return jnp.broadcast_to(values[entry : entry + 1, :], zero.shape)

    codes = [spread(code, entry) for entry in range(listed)]
    locals_ = [spread(local, entry) for entry in range(listed)]
    couplings = [spread(coupling, entry) for entry in range(listed)]
    shade = jnp.broadcast_to(colour[...], zero.shape)

    def block_wait(step, carry):
        source = lax.rem(me + tiles * STRIDE - step * STRIDE, tiles)
        pltpu.make_async_remote_copy(
            src_ref=outgoing.at[pl.ds(source * cap, cap)],
            dst_ref=arrived.at[pl.ds(source * cap, cap)],
            send_sem=block_send.at[source],
            recv_sem=block_recv.at[source],
            device_id={"tile": source},
            device_id_type=MESH,
        ).wait()
        return carry

    lax.fori_loop(1, tiles, block_wait, 0)

    def project(step, total):
        for inner in range(unroll):
            comp = step * unroll + inner
            weights = footprint[comp].astype(jnp.float32)
            products = jnp.zeros((frames_dev, voxels), jnp.float32)
            for entry in range(blocks_fp):
                block = arrived[slots[entry, comp]].astype(jnp.float32)
                products = products + block * weights[entry : entry + 1, :]
            column = jnp.sum(products, axis=1, keepdims=True)
            total = jnp.where(lane == comp, column, total)
        return total

    projected = lax.fori_loop(0, comps // unroll, project, zero)

    current = init[...]
    for step_colour in range(COLOURS):
        for copy in copies:
            copy.wait()
        sides = [table[step_colour, region] for region in range(3)]
        neighbour_sum = zero
        for entry in range(listed):
            index = locals_[entry]
            picked = jnp.take_along_axis(current, index, axis=1)
            for region in range(3):
                side = jnp.take_along_axis(sides[region], index, axis=1)
                picked = jnp.where(codes[entry] == region, side, picked)
            neighbour_sum = neighbour_sum + couplings[entry] * picked
        fresh = jnp.maximum((projected - neighbour_sum) / self_gram, 0.0)
        current = jnp.where(shade == step_colour, fresh, current)
        if step_colour + 1 < COLOURS:
            mine[step_colour] = current
            copies = near_copies(mine.at[step_colour], step_colour + 1)
            for copy in copies:
                copy.start()
    traces_out[...] = current

    parts[row] = jnp.sum(current * current, axis=0, keepdims=True)

    def part_start(step, carry):
        peer = lax.rem(row + step, groups)
        pltpu.make_async_remote_copy(
            src_ref=parts.at[row],
            dst_ref=parts.at[row],
            send_sem=part_send.at[peer],
            recv_sem=part_recv.at[row],
            device_id={"tm": peer},
            device_id_type=MESH,
        ).start()
        return carry

    def part_wait(step, carry):
        source = lax.rem(row + step, groups)
        pltpu.make_async_remote_copy(
            src_ref=parts.at[source],
            dst_ref=parts.at[source],
            send_sem=part_send.at[source],
            recv_sem=part_recv.at[source],
            device_id={"tm": source},
            device_id_type=MESH,
        ).wait()
        return carry

    lax.fori_loop(1, groups, part_start, 0)
    lax.fori_loop(1, groups, part_wait, 0)
    energy = parts[0]
    for group in range(1, groups):
        energy = energy + parts[group]
    rms_out[...] = jnp.sqrt(energy / (frames_dev * groups) + 1e-06)


def shards(
    tiles, groups, data, send_list, footprint_slot, footprint, colour, correlation, correlation_gram, traces_init
):
    comps = colour.shape[0]
    frames_dev, voxels = data.shape[1:]
    cap = send_list.shape[2]
    vmem = pl.BlockSpec(memory_space=pltpu.VMEM)
    smem = pl.BlockSpec(memory_space=pltpu.SMEM)
    traces, trace_rms = pl.pallas_call(
        functools.partial(sweep_kernel, tiles, groups),
        out_shape=(
            jax.ShapeDtypeStruct((frames_dev, comps), jnp.float32),
            jax.ShapeDtypeStruct((1, comps), jnp.float32),
        ),
        in_specs=[vmem, smem, smem, vmem, vmem, vmem, vmem, vmem],
        out_specs=(vmem, vmem),
        scratch_shapes=[
            pltpu.VMEM((tiles * cap, frames_dev, voxels), data.dtype),
            pltpu.VMEM((tiles * cap, frames_dev, voxels), data.dtype),
            pltpu.VMEM((COLOURS, 3, frames_dev, comps), jnp.float32),
            pltpu.VMEM((COLOURS - 1, frames_dev, comps), jnp.float32),
            pltpu.VMEM((groups, 1, comps), jnp.float32),
            pltpu.SemaphoreType.DMA((tiles,)),
            pltpu.SemaphoreType.DMA((tiles,)),
            pltpu.SemaphoreType.DMA((COLOURS, 3)),
            pltpu.SemaphoreType.DMA((COLOURS, 3)),
            pltpu.SemaphoreType.DMA((groups,)),
            pltpu.SemaphoreType.DMA((groups,)),
        ],
        compiler_params=pltpu.CompilerParams(collective_id=0, has_side_effects=True),
        name="trace_sweep",
    )(
        data,
        send_list[0].T,
        footprint_slot.T,
        footprint,
        colour.reshape(1, comps),
        correlation.T,
        correlation_gram.T,
        traces_init,
    )
    return traces, trace_rms.reshape(comps)


def solution(mesh):
    placed = (
        P("tile", "tm", None),
        P("tile", None, None),
        P("tile", None),
        P("tile", None, None),
        P("tile"),
        P("tile", None),
        P("tile", None),
        P("tm", "tile"),
    )
    return jax.shard_map(
        functools.partial(shards, mesh.shape["tile"], mesh.shape["tm"]),
        mesh=mesh,
        in_specs=placed,
        out_specs=(P("tm", "tile"), P("tile")),
        check_vma=False,
    )
```

```python
import functools

import jax
import jax.numpy as jnp
from jax import lax
from jax.experimental import pallas as pl
from jax.experimental.pallas import tpu as pltpu
from jax.sharding import PartitionSpec as P

MESH = pl.DeviceIdType.MESH
INNER = 8


def offsets_within(tiles):
    half = tiles // 2
    reach = {0}
    rings = []
    for _ in range(3):
        reach = {(at + move) % tiles for at in reach for move in (0, 1, -1, half)}
        rings.append(reach)
    first, second, third = rings
    close = sorted(second - {0})
    return sorted(first), close, close + sorted(third - second)


def sweep_kernel(
    tiles, groups, data, send, slots, footprint, colour, correlation, gram, init,
    traces_out, energy_out, outgoing, arrived, near_init, near_ids, near_gram, near_rows,
    rows, mixed, near_mixed, parts,
    block_send, block_recv, near_send, near_recv, mixed_send, mixed_recv, part_send, part_recv,
):
    me = lax.axis_index("tile")
    row = lax.axis_index("tm")
    cap = send.shape[0]
    blocks_fp, comps = slots.shape
    frames_dev, voxels = data.shape[1:]
    listed = correlation.shape[0]
    half = tiles // 2
    inner_count = min(INNER, tiles)
    outer_count = tiles // inner_count
    outer_half = outer_count // 2
    outer = me // inner_count
    inner = lax.rem(me, inner_count)
    adjacent, close, reached = offsets_within(tiles)

    barrier = pltpu.get_barrier_semaphore()

    def greet_tile(step, carry):
        peer = lax.rem(me + step, tiles)
        pl.semaphore_signal(barrier, inc=1, device_id={"tile": peer}, device_id_type=MESH)
        return carry

    def greet_row(step, carry):
        peer = lax.rem(row + step, groups)
        pl.semaphore_signal(barrier, inc=1, device_id={"tm": peer}, device_id_type=MESH)
        return carry

    lax.fori_loop(1, tiles, greet_tile, 0)
    lax.fori_loop(1, groups, greet_row, 0)

    def collect(owner, carry):
        for slot in range(cap):
            outgoing[owner * cap + slot] = data[send[slot, owner]]
        return carry

    lax.fori_loop(0, tiles, collect, 0)
    for slot in range(cap):
        arrived[me * cap + slot] = outgoing[me * cap + slot]

    pl.semaphore_wait(barrier, tiles - 1 + groups - 1)

    def block_start(outer_step, inner_step):
        peer = lax.rem(outer + outer_step, outer_count) * inner_count + lax.rem(inner + inner_step, inner_count)
        pltpu.make_async_remote_copy(
            src_ref=outgoing.at[pl.ds(peer * cap, cap)],
            dst_ref=arrived.at[pl.ds(me * cap, cap)],
            send_sem=block_send.at[peer],
            recv_sem=block_recv.at[me],
            device_id={"tile": peer},
            device_id_type=MESH,
        ).start()

    def opposite_start(step, carry):
        block_start(outer_half, step)
        return carry

    def paired_start(step, carry):
        distance = outer_half - 1 - step // (2 * inner_count)
        within = lax.rem(step, 2 * inner_count)
        way = lax.rem(within, 2)
        block_start(distance + way * (outer_count - 2 * distance), within // 2)
        return carry

    def local_start(step, carry):
        block_start(0, step)
        return carry

    if outer_count > 1:
        lax.fori_loop(0, inner_count, opposite_start, 0)
        lax.fori_loop(0, (outer_half - 1) * 2 * inner_count, paired_start, 0)
    lax.fori_loop(1, inner_count, local_start, 0)

    lane = lax.broadcasted_iota(jnp.int32, (frames_dev, comps), 1)
    zero = jnp.zeros((frames_dev, comps), jnp.float32)
    unroll = 8

    def square(step, total):
        for within in range(unroll):
            comp = step * unroll + within
            weights = footprint[comp].astype(jnp.float32)
            column = jnp.sum(weights * weights, axis=1, keepdims=True)
            total = jnp.where(lane == comp, column, total)
        return total

    squares = lax.fori_loop(0, comps // unroll, square, zero)
    rows[0:1, :] = jnp.sum(squares, axis=0, keepdims=True)
    rows[1:2, :] = colour[...].astype(jnp.float32)

    def near_copies(offset):
        peer = lax.rem(me + offset, tiles)
        place = close.index((tiles - offset) % tiles)
        return [
            pltpu.make_async_remote_copy(
                src_ref=source,
                dst_ref=target.at[place],
                send_sem=near_send.at[kind, place],
                recv_sem=near_recv.at[kind, place],
                device_id={"tile": peer},
                device_id_type=MESH,
            )
            for kind, (source, target) in enumerate(
                ((init, near_init), (correlation, near_ids), (gram, near_gram), (rows, near_rows))
            )
        ]

    statics = {offset: near_copies(offset) for offset in close}
    for kind in range(4):
        for offset in close:
            statics[offset][kind].start()

    def block_wait(step, carry):
        source = lax.rem(me + step, tiles)
        pltpu.make_async_remote_copy(
            src_ref=outgoing.at[pl.ds(source * cap, cap)],
            dst_ref=arrived.at[pl.ds(source * cap, cap)],
            send_sem=block_send.at[source],
            recv_sem=block_recv.at[source],
            device_id={"tile": source},
            device_id_type=MESH,
        ).wait()
        return carry

    lax.fori_loop(1, tiles, block_wait, 0)

    def project(step, total):
        for within in range(unroll):
            comp = step * unroll + within
            weights = footprint[comp].astype(jnp.float32)
            products = jnp.zeros((frames_dev, voxels), jnp.float32)
            for entry in range(blocks_fp):
                block = arrived[slots[entry, comp]].astype(jnp.float32)
                products = products + block * weights[entry : entry + 1, :]
            column = jnp.sum(products, axis=1, keepdims=True)
            total = jnp.where(lane == comp, column, total)
        return total

    projected = lax.fori_loop(0, comps // unroll, project, zero)

    def update(offset, step_colour, values, sums, ids, weights, energy, shade):
        around = [values[(offset + move) % tiles] for move in (1, tiles - 1, half, 0)]
        owner = lax.shift_right_logical(ids, comps.bit_length() - 1)
        local = ids & (comps - 1)
        code = jnp.where(owner == lax.rem(me + offset + half, tiles), 2, 3)
        code = jnp.where(owner == lax.rem(me + offset + tiles - 1, tiles), 1, code)
        code = jnp.where(owner == lax.rem(me + offset + 1, tiles), 0, code)
        neighbour_sum = zero
        for entry in range(listed):
            index = jnp.broadcast_to(local[entry : entry + 1, :], zero.shape)
            which = jnp.broadcast_to(code[entry : entry + 1, :], zero.shape)
            weight = jnp.broadcast_to(weights[entry : entry + 1, :], zero.shape)
            picked = jnp.take_along_axis(around[3], index, axis=1)
            for region in range(3):
                side = jnp.take_along_axis(around[region], index, axis=1)
                picked = jnp.where(which == region, side, picked)
            neighbour_sum = neighbour_sum + weight * picked
        fresh = jnp.maximum((sums - neighbour_sum) / energy, 0.0)
        return jnp.where(shade == step_colour, fresh, values[offset])

    def waited(offset, kind):
        copy = statics[(tiles - offset) % tiles][kind]
        copy.wait()

    facts = {0: (correlation[...], gram[...], rows[0:1, :], rows[1:2, :].astype(jnp.int32))}
    for offset in close:
        waited(offset, 0)
    starts = {offset: near_init[place] for place, offset in enumerate(close)}
    starts[0] = init[...]
    values = {0: update(0, 0, starts, projected, *facts[0])}
    mixed[0] = jnp.where(facts[0][3] == 0, values[0], projected)
    mixed[1] = values[0]
    mixes = []
    for offset in reversed(reached):
        place = reached.index((tiles - offset) % tiles)
        mixes.append(
            pltpu.make_async_remote_copy(
                src_ref=mixed.at[0 if offset in close else 1],
                dst_ref=near_mixed.at[place],
                send_sem=mixed_send.at[place],
                recv_sem=mixed_recv.at[place],
                device_id={"tile": lax.rem(me + offset, tiles)},
                device_id_type=MESH,
            )
        )
    for copy in mixes:
        copy.start()
    for offset in close:
        for kind in range(1, 4):
            waited(offset, kind)
    for place, offset in enumerate(close):
        facts[offset] = (
            near_ids[place],
            near_gram[place],
            near_rows[place, 0:1, :],
            near_rows[place, 1:2, :].astype(jnp.int32),
        )
    for copy in mixes:
        copy.wait()

    sums = {0: projected}
    for place, offset in enumerate(reached):
        values[offset] = near_mixed[place]
    for offset in close:
        sums[offset] = values[offset]
        values[offset] = jnp.where(facts[offset][3] == 0, sums[offset], starts[offset])
    for step_colour, area in ((1, [0] + close), (2, adjacent), (3, [0])):
        renewed = {offset: update(offset, step_colour, values, sums[offset], *facts[offset]) for offset in area}
        values = renewed
    current = values[0]
    traces_out[...] = current

    parts[row] = jnp.sum(current * current, axis=0, keepdims=True)

    def part_start(step, carry):
        peer = lax.rem(row + step, groups)
        pltpu.make_async_remote_copy(
            src_ref=parts.at[row],
            dst_ref=parts.at[row],
            send_sem=part_send.at[peer],
            recv_sem=part_recv.at[row],
            device_id={"tm": peer},
            device_id_type=MESH,
        ).start()
        return carry

    def part_wait(step, carry):
        source = lax.rem(row + step, groups)
        pltpu.make_async_remote_copy(
            src_ref=parts.at[source],
            dst_ref=parts.at[source],
            send_sem=part_send.at[source],
            recv_sem=part_recv.at[source],
            device_id={"tm": source},
            device_id_type=MESH,
        ).wait()
        return carry

    lax.fori_loop(1, groups, part_start, 0)
    lax.fori_loop(1, groups, part_wait, 0)
    energy = parts[0]
    for group in range(1, groups):
        energy = energy + parts[group]
    energy_out[...] = energy


def shards(
    tiles, groups, data, send_list, footprint_slot, footprint, colour, correlation, correlation_gram, traces_init
):
    comps = colour.shape[0]
    frames_dev, voxels = data.shape[1:]
    cap = send_list.shape[2]
    vmem = pl.BlockSpec(memory_space=pltpu.VMEM)
    smem = pl.BlockSpec(memory_space=pltpu.SMEM)
    _, close, reached = offsets_within(tiles)
    tile_shape = (frames_dev, comps)
    list_shape = (correlation.shape[1], comps)
    traces, energy = pl.pallas_call(
        functools.partial(sweep_kernel, tiles, groups),
        out_shape=(
            jax.ShapeDtypeStruct((frames_dev, comps), jnp.float32),
            jax.ShapeDtypeStruct((1, comps), jnp.float32),
        ),
        in_specs=[vmem, smem, smem, vmem, vmem, vmem, vmem, vmem],
        out_specs=(vmem, vmem),
        scratch_shapes=[
            pltpu.VMEM((tiles * cap, frames_dev, voxels), data.dtype),
            pltpu.VMEM((tiles * cap, frames_dev, voxels), data.dtype),
            pltpu.VMEM((len(close),) + tile_shape, jnp.float32),
            pltpu.VMEM((len(close),) + list_shape, jnp.int32),
            pltpu.VMEM((len(close),) + list_shape, jnp.float32),
            pltpu.VMEM((len(close), 2, comps), jnp.float32),
            pltpu.VMEM((2, comps), jnp.float32),
            pltpu.VMEM((2,) + tile_shape, jnp.float32),
            pltpu.VMEM((len(reached),) + tile_shape, jnp.float32),
            pltpu.VMEM((groups, 1, comps), jnp.float32),
            pltpu.SemaphoreType.DMA((tiles,)),
            pltpu.SemaphoreType.DMA((tiles,)),
            pltpu.SemaphoreType.DMA((4, len(close))),
            pltpu.SemaphoreType.DMA((4, len(close))),
            pltpu.SemaphoreType.DMA((len(reached),)),
            pltpu.SemaphoreType.DMA((len(reached),)),
            pltpu.SemaphoreType.DMA((groups,)),
            pltpu.SemaphoreType.DMA((groups,)),
        ],
        compiler_params=pltpu.CompilerParams(collective_id=0, has_side_effects=True),
        name="trace_sweep",
    )(
        data,
        send_list[0].T,
        footprint_slot.T,
        footprint,
        colour.reshape(1, comps),
        correlation.T,
        correlation_gram.T,
        traces_init,
    )
    trace_rms = jnp.sqrt(energy.reshape(comps) / (frames_dev * groups) + 1e-06)
    return jnp.maximum(traces, 0.0), trace_rms


def solution(mesh):
    placed = (
        P("tile", "tm", None),
        P("tile", None, None),
        P("tile", None),
        P("tile", None, None),
        P("tile"),
        P("tile", None),
        P("tile", None),
        P("tm", "tile"),
    )
    return jax.shard_map(
        functools.partial(shards, mesh.shape["tile"], mesh.shape["tm"]),
        mesh=mesh,
        in_specs=placed,
        out_specs=(P("tm", "tile"), P("tile")),
        check_vma=False,
    )
```

```python
import functools

import jax
import jax.numpy as jnp
from jax import lax
from jax.experimental import pallas as pl
from jax.experimental.pallas import tpu as pltpu
from jax.sharding import PartitionSpec as P

MESH = pl.DeviceIdType.MESH
INNER = 8


def offsets_within(tiles):
    half = tiles // 2
    reach = {0}
    rings = []
    for _ in range(3):
        reach = {(at + move) % tiles for at in reach for move in (0, 1, -1, half)}
        rings.append(reach)
    first, second, third = rings
    close = sorted(second - {0})
    return sorted(first), close, close + sorted(third - second)


def sweep_kernel(
    tiles, groups, data_in, send_in, slots_in, footprint_in, colour_in, correlation_in, gram_in, init_in,
    traces_out, energy_out, data, send, slots, footprint, colour, correlation, gram, init, load_sem,
    wide_blocks, wide_weights, outgoing, arrived, near_init, near_ids, near_gram, near_rows,
    rows, mixed, near_mixed, parts,
    block_send, block_recv, near_send, near_recv, mixed_send, mixed_recv, part_send, part_recv,
):
    me = lax.axis_index("tile")
    row = lax.axis_index("tm")
    cap = send.shape[0]
    blocks_fp, comps = slots.shape
    frames_dev, voxels = data.shape[1:]
    listed = correlation.shape[0]
    half = tiles // 2
    inner_count = min(INNER, tiles)
    outer_count = tiles // inner_count
    outer_half = outer_count // 2
    outer = me // inner_count
    inner = lax.rem(me, inner_count)
    adjacent, close, reached = offsets_within(tiles)

    barrier = pltpu.get_barrier_semaphore()

    def greet_tile(step, carry):
        peer = lax.rem(me + step, tiles)
        pl.semaphore_signal(barrier, inc=1, device_id={"tile": peer}, device_id_type=MESH)
        return carry

    def greet_row(step, carry):
        peer = lax.rem(row + step, groups)
        pl.semaphore_signal(barrier, inc=1, device_id={"tm": peer}, device_id_type=MESH)
        return carry

    lax.fori_loop(1, tiles, greet_tile, 0)
    lax.fori_loop(1, groups, greet_row, 0)

    loads = [
        pltpu.make_async_copy(source, target, load_sem.at[place])
        for place, (source, target) in enumerate(
            (
                (data_in, data), (send_in, send), (footprint_in, footprint), (init_in, init),
                (colour_in, colour), (correlation_in, correlation), (gram_in, gram), (slots_in, slots),
            )
        )
    ]
    for load in loads:
        load.start()
    for load in loads[:2]:
        load.wait()

    def collect(owner, carry):
        for slot in range(cap):
            outgoing[owner * cap + slot] = data[send[slot, owner]]
        return carry

    lax.fori_loop(0, tiles, collect, 0)
    for slot in range(cap):
        wide_blocks[me * cap + slot] = outgoing[me * cap + slot].astype(jnp.float32)
    for load in loads[2:]:
        load.wait()

    pl.semaphore_wait(barrier, tiles - 1 + groups - 1)

    def tile_at(outer_step, inner_step):
        return lax.rem(outer + outer_step, outer_count) * inner_count + lax.rem(inner + inner_step, inner_count)

    def every_pair(act):
        def opposite(step, carry):
            act(outer_half, step)
            return carry

        def paired(step, carry):
            distance = outer_half - 1 - step // (2 * inner_count)
            within = lax.rem(step, 2 * inner_count)
            way = lax.rem(within, 2)
            act(distance + way * (outer_count - 2 * distance), within // 2)
            return carry

        def local(step, carry):
            act(0, step)
            return carry

        if outer_count > 1:
            lax.fori_loop(0, inner_count, opposite, 0)
            lax.fori_loop(0, (outer_half - 1) * 2 * inner_count, paired, 0)
        lax.fori_loop(1, inner_count, local, 0)

    def block_start(outer_step, inner_step):
        peer = tile_at(outer_step, inner_step)
        pltpu.make_async_remote_copy(
            src_ref=outgoing.at[pl.ds(peer * cap, cap)],
            dst_ref=arrived.at[pl.ds(me * cap, cap)],
            send_sem=block_send.at[peer],
            recv_sem=block_recv.at[me],
            device_id={"tile": peer},
            device_id_type=MESH,
        ).start()

    every_pair(block_start)

    lane = lax.broadcasted_iota(jnp.int32, (frames_dev, comps), 1)
    zero = jnp.zeros((frames_dev, comps), jnp.float32)
    unroll = 16

    def square(step, total):
        for within in range(unroll):
            comp = step * unroll + within
            weights = footprint[comp].astype(jnp.float32)
            wide_weights[pl.ds(pl.multiple_of(comp * blocks_fp, blocks_fp), blocks_fp), :] = weights
            column = jnp.sum(weights * weights, axis=1, keepdims=True)
            total = jnp.where(lane == comp, column, total)
        return total

    squares = lax.fori_loop(0, comps // unroll, square, zero)
    rows[0:1, :] = jnp.sum(squares, axis=0, keepdims=True)
    rows[1:2, :] = colour[...].astype(jnp.float32)

    def near_copies(offset):
        peer = lax.rem(me + offset, tiles)
        place = close.index((tiles - offset) % tiles)
        return [
            pltpu.make_async_remote_copy(
                src_ref=source,
                dst_ref=target.at[place],
                send_sem=near_send.at[kind, place],
                recv_sem=near_recv.at[kind, place],
                device_id={"tile": peer},
                device_id_type=MESH,
            )
            for kind, (source, target) in enumerate(
                ((init, near_init), (correlation, near_ids), (gram, near_gram), (rows, near_rows))
            )
        ]

    statics = {offset: near_copies(offset) for offset in close}
    for kind in range(4):
        for offset in close:
            statics[offset][kind].start()

    def block_wait(outer_step, inner_step):
        source = tile_at(outer_step, inner_step)
        pltpu.make_async_remote_copy(
            src_ref=outgoing.at[pl.ds(source * cap, cap)],
            dst_ref=arrived.at[pl.ds(source * cap, cap)],
            send_sem=block_send.at[source],
            recv_sem=block_recv.at[source],
            device_id={"tile": source},
            device_id_type=MESH,
        ).wait()
        for slot in range(cap):
            wide_blocks[source * cap + slot] = arrived[source * cap + slot].astype(jnp.float32)

    every_pair(block_wait)

    def project(step, total):
        for within in range(unroll):
            comp = step * unroll + within
            products = jnp.zeros((frames_dev, voxels), jnp.float32)
            for entry in range(blocks_fp):
                weights = wide_weights[pl.ds(comp * blocks_fp + entry, 1), :]
                products = products + wide_blocks[slots[entry, comp]] * weights
            column = jnp.sum(products, axis=1, keepdims=True)
            total = jnp.where(lane == comp, column, total)
        return total

    projected = lax.fori_loop(0, comps // unroll, project, zero)

    def update(offset, step_colour, values, sums, ids, weights, energy, shade):
        around = [values[(offset + move) % tiles] for move in (1, tiles - 1, half, 0)]
        owner = lax.shift_right_logical(ids, comps.bit_length() - 1)
        local = ids & (comps - 1)
        code = jnp.where(owner == lax.rem(me + offset + half, tiles), 2, 3)
        code = jnp.where(owner == lax.rem(me + offset + tiles - 1, tiles), 1, code)
        code = jnp.where(owner == lax.rem(me + offset + 1, tiles), 0, code)
        neighbour_sum = zero
        for entry in range(listed):
            index = jnp.broadcast_to(local[entry : entry + 1, :], zero.shape)
            which = jnp.broadcast_to(code[entry : entry + 1, :], zero.shape)
            weight = jnp.broadcast_to(weights[entry : entry + 1, :], zero.shape)
            picked = jnp.take_along_axis(around[3], index, axis=1)
            for region in range(3):
                side = jnp.take_along_axis(around[region], index, axis=1)
                picked = jnp.where(which == region, side, picked)
            neighbour_sum = neighbour_sum + weight * picked
        fresh = jnp.maximum((sums - neighbour_sum) / energy, 0.0)
        return jnp.where(shade == step_colour, fresh, values[offset])

    def waited(offset, kind):
        copy = statics[(tiles - offset) % tiles][kind]
        copy.wait()

    facts = {0: (correlation[...], gram[...], rows[0:1, :], rows[1:2, :].astype(jnp.int32))}
    for offset in close:
        waited(offset, 0)
    starts = {offset: near_init[place] for place, offset in enumerate(close)}
    starts[0] = init[...]
    values = {0: update(0, 0, starts, projected, *facts[0])}
    mixed[0] = jnp.where(facts[0][3] == 0, values[0], projected)
    mixed[1] = values[0]
    mixes = []
    for offset in reversed(reached):
        place = reached.index((tiles - offset) % tiles)
        mixes.append(
            pltpu.make_async_remote_copy(
                src_ref=mixed.at[0 if offset in close else 1],
                dst_ref=near_mixed.at[place],
                send_sem=mixed_send.at[place],
                recv_sem=mixed_recv.at[place],
                device_id={"tile": lax.rem(me + offset, tiles)},
                device_id_type=MESH,
            )
        )
    for copy in mixes:
        copy.start()
    for offset in close:
        for kind in range(1, 4):
            waited(offset, kind)
    for place, offset in enumerate(close):
        facts[offset] = (
            near_ids[place],
            near_gram[place],
            near_rows[place, 0:1, :],
            near_rows[place, 1:2, :].astype(jnp.int32),
        )
    for copy in mixes:
        copy.wait()

    sums = {0: projected}
    for place, offset in enumerate(reached):
        values[offset] = near_mixed[place]
    for offset in close:
        sums[offset] = values[offset]
        values[offset] = jnp.where(facts[offset][3] == 0, sums[offset], starts[offset])
    for step_colour, area in ((1, [0] + close), (2, adjacent), (3, [0])):
        renewed = {offset: update(offset, step_colour, values, sums[offset], *facts[offset]) for offset in area}
        values = renewed
    current = values[0]
    traces_out[...] = current

    parts[row] = jnp.sum(current * current, axis=0, keepdims=True)

    def part_start(step, carry):
        peer = lax.rem(row + step, groups)
        pltpu.make_async_remote_copy(
            src_ref=parts.at[row],
            dst_ref=parts.at[row],
            send_sem=part_send.at[peer],
            recv_sem=part_recv.at[row],
            device_id={"tm": peer},
            device_id_type=MESH,
        ).start()
        return carry

    def part_wait(step, carry):
        source = lax.rem(row + step, groups)
        pltpu.make_async_remote_copy(
            src_ref=parts.at[source],
            dst_ref=parts.at[source],
            send_sem=part_send.at[source],
            recv_sem=part_recv.at[source],
            device_id={"tm": source},
            device_id_type=MESH,
        ).wait()
        return carry

    lax.fori_loop(1, groups, part_start, 0)
    lax.fori_loop(1, groups, part_wait, 0)
    energy = parts[0]
    for group in range(1, groups):
        energy = energy + parts[group]
    energy_out[...] = energy


def shards(
    tiles, groups, data, send_list, footprint_slot, footprint, colour, correlation, correlation_gram, traces_init
):
    comps = colour.shape[0]
    frames_dev, voxels = data.shape[1:]
    cap = send_list.shape[2]
    vmem = pl.BlockSpec(memory_space=pltpu.VMEM)
    anywhere = pl.BlockSpec(memory_space=pl.ANY)
    slot_total, blocks_fp = tiles * cap, footprint.shape[1]
    _, close, reached = offsets_within(tiles)
    tile_shape = (frames_dev, comps)
    list_shape = (correlation.shape[1], comps)
    traces, energy = pl.pallas_call(
        functools.partial(sweep_kernel, tiles, groups),
        out_shape=(
            jax.ShapeDtypeStruct((frames_dev, comps), jnp.float32),
            jax.ShapeDtypeStruct((1, comps), jnp.float32),
        ),
        in_specs=[anywhere] * 8,
        out_specs=(vmem, vmem),
        scratch_shapes=[
            pltpu.VMEM(data.shape, data.dtype),
            pltpu.SMEM((cap, tiles), jnp.int32),
            pltpu.SMEM((blocks_fp, comps), jnp.int32),
            pltpu.VMEM(footprint.shape, footprint.dtype),
            pltpu.VMEM((1, comps), jnp.int32),
            pltpu.VMEM(list_shape, jnp.int32),
            pltpu.VMEM(list_shape, jnp.float32),
            pltpu.VMEM(tile_shape, jnp.float32),
            pltpu.SemaphoreType.DMA((8,)),
            pltpu.VMEM((slot_total, frames_dev, voxels), jnp.float32),
            pltpu.VMEM((comps * blocks_fp, voxels), jnp.float32),
            pltpu.VMEM((tiles * cap, frames_dev, voxels), data.dtype),
            pltpu.VMEM((tiles * cap, frames_dev, voxels), data.dtype),
            pltpu.VMEM((len(close),) + tile_shape, jnp.float32),
            pltpu.VMEM((len(close),) + list_shape, jnp.int32),
            pltpu.VMEM((len(close),) + list_shape, jnp.float32),
            pltpu.VMEM((len(close), 2, comps), jnp.float32),
            pltpu.VMEM((2, comps), jnp.float32),
            pltpu.VMEM((2,) + tile_shape, jnp.float32),
            pltpu.VMEM((len(reached),) + tile_shape, jnp.float32),
            pltpu.VMEM((groups, 1, comps), jnp.float32),
            pltpu.SemaphoreType.DMA((tiles,)),
            pltpu.SemaphoreType.DMA((tiles,)),
            pltpu.SemaphoreType.DMA((4, len(close))),
            pltpu.SemaphoreType.DMA((4, len(close))),
            pltpu.SemaphoreType.DMA((len(reached),)),
            pltpu.SemaphoreType.DMA((len(reached),)),
            pltpu.SemaphoreType.DMA((groups,)),
            pltpu.SemaphoreType.DMA((groups,)),
        ],
        compiler_params=pltpu.CompilerParams(collective_id=0, has_side_effects=True),
        name="trace_sweep",
    )(
        data,
        send_list[0].T,
        footprint_slot.T,
        footprint,
        colour.reshape(1, comps),
        correlation.T,
        correlation_gram.T,
        traces_init,
    )
    trace_rms = jnp.sqrt(energy.reshape(comps) / (frames_dev * groups) + 1e-06)
    return jnp.maximum(traces, 0.0), trace_rms


def solution(mesh):
    placed = (
        P("tile", "tm", None),
        P("tile", None, None),
        P("tile", None),
        P("tile", None, None),
        P("tile"),
        P("tile", None),
        P("tile", None),
        P("tm", "tile"),
    )
    return jax.shard_map(
        functools.partial(shards, mesh.shape["tile"], mesh.shape["tm"]),
        mesh=mesh,
        in_specs=placed,
        out_specs=(P("tm", "tile"), P("tile")),
        check_vma=False,
    )
```
